32 devices in a mesh: groups: 2 (over y), feat: 8 (over z, x), corp: 2 (over core).
Axes of the slice: x: 2, y: 2, z: 4, core: 2. Of those that a mesh axis runs over, the one named last changes fastest.
Arguments:
- query_features: bfloat16 [1536, 16384], P(('groups', 'corp'), 'feat'), parts along dimension 0, may hold values from -6 to 6
- inverse_kernel: bfloat16 [16384, 16384], P(None, 'feat'), may hold values from -1 to 3, as said below
- doc_features: bfloat16 [512, 16384], P(('groups', 'corp'), 'feat'), parts along dimension 0, may hold values from -0.046875 to 0.046875
Outputs:
- scores: float32 [1536, 256], P(('groups', 'feat'), 'corp'), parts along dimension 0
The draws below stay inside these ranges and needn't reach their ends.
There are 2 independent parts, one for each index of `groups`. The reference program is written for one: setup_inputs(seed, part) draws one part's arguments, and reference() takes and returns one part's arrays. A program takes and returns all parts, laid end to end along the dimension named above; an argument that names none is the same for every part. Nothing has to cross between parts.
Inputs may be any that keep to these rules, and one draw needn't show every extreme that they name: inverse_kernel is symmetric.
All inputs are finite; a program needn't handle non-finite values.
Results may differ from the reference program's by a relative error of at most 0.0003.
Values may be sent and summed in bfloat16 or wider, within the bound.
No kernel may reach another device: no remote copies, remote signals or barrier semaphores. Data moves between devices by JAX's collectives and lax.ppermute only.
A program may use at most 128 MiB of HBM per device.

```python
import math
import jax
import jax.numpy as jnp
from jax import lax

K = 16384
QUERIES = 768
DOCS = 256


def draw_inverse_kernel(key, part):
    noise_key, diag_key = jax.random.split(key)
    noise = jnp.clip(jax.random.normal(noise_key, (K, K), jnp.float32), -4.0, 4.0)
    diag_values = 0.5 + 2.0 * jax.random.uniform(diag_key, (K,), jnp.float32)
    symmetric = (noise + noise.T) * (math.sqrt(0.5) / math.sqrt(K))
    row_index = iota_rows()
    diagonal_mask = row_index == row_index.T
    return jnp.where(diagonal_mask, diag_values[None, :], symmetric).astype(jnp.bfloat16)


def iota_rows():
    return jnp.arange(K, dtype=jnp.int32)[:, None] + jnp.zeros((1, K), jnp.int32)


def levels(key, extent, cuts, low, largest):
    def one(position, blocks):
        heights = jax.random.uniform(jax.random.fold_in(jax.random.fold_in(key, 6), position), (blocks,), jnp.float32, low / len(cuts), largest / len(cuts))
        return jnp.repeat(jnp.exp(heights), extent[position] // blocks).reshape((-1,) + (1,) * (len(extent) - position - 1))

    gain = one(*cuts[0])
    for cut in cuts[1:]:
        gain = gain * one(*cut)
    return gain


def centred(key, dims, spread, most, shards=(), kind=jnp.bfloat16):
    level = levels(key, dims, shards, -0.22, 0.18) if shards else 1.0
    array = jax.random.normal(key, dims, jnp.float32) * spread * level
    return jnp.minimum(jnp.maximum(array, -most), most).astype(kind)


def setup_inputs(seed: int = 0, part: int = 0) -> dict:
    arg_keys = jax.random.split(jax.random.key(seed), 4)
    part_keys = jax.random.split(jax.random.fold_in(arg_keys[3], part), 4)
    query_features = centred(part_keys[0], (QUERIES, K), 1.0, 6.0, ((0, 2), (1, 8)))
    inverse_kernel = draw_inverse_kernel(jax.random.fold_in(arg_keys[3], 71), part)
    doc_features = centred(part_keys[2], (DOCS, K), K ** -0.5, 0.046875, ((0, 2), (1, 8)))
    return dict(query_features=query_features, inverse_kernel=inverse_kernel, doc_features=doc_features)


def reference(query_features, inverse_kernel, doc_features):
    precond = jnp.dot(query_features, inverse_kernel, preferred_element_type=jnp.float32)
    return jnp.dot(precond, doc_features.astype(jnp.float32).T, precision=lax.Precision.HIGHEST)
```

```python
import jax
import jax.numpy as jnp
from jax import lax
from jax.sharding import PartitionSpec as P

F32 = jnp.float32
BF16 = jnp.bfloat16


def dot(a, b):
    return jnp.dot(a, b, preferred_element_type=F32)


def dot_t(a, b):
    return lax.dot_general(a, b, (((1,), (1,)), ((), ())), preferred_element_type=F32)


def gather_rows(x, axis, n):
    me = lax.axis_index(axis)
    out = jnp.zeros((n,) + x.shape, x.dtype)
    out = lax.dynamic_update_index_in_dim(out, x, me, 0)
    for k in range(1, n):
        y = lax.ppermute(x, axis, [(i, (i + k) % n) for i in range(n)])
        out = lax.dynamic_update_index_in_dim(out, y, (me + n - k) % n, 0)
    return out.reshape((n * x.shape[0],) + x.shape[1:])


def scatter_sum(s, n):
    me = lax.axis_index("feat")
    x, z, m = me % 2, me // 2, n // 2
    s = s.reshape((m, 2) + s.shape[1:])
    mine = lax.dynamic_index_in_dim(s, x, 1, False)
    theirs = lax.dynamic_index_in_dim(s, 1 - x, 1, False)
    s = mine + lax.ppermute(theirs, "feat", [(i, i ^ 1) for i in range(n)])
    out = lax.dynamic_index_in_dim(s, z, 0, False)
    for k in range(1, m):
        y = lax.dynamic_index_in_dim(s, (z + k) % m, 0, False)
        out = out + lax.ppermute(y, "feat", [(i, (i + 2 * k) % n) for i in range(n)])
    return out


def split(a):
    hi = lax.reduce_precision(a, 8, 7)
    return hi.astype(BF16), (a - hi).astype(BF16)


def ring_body(n, n_corp, q, m, d):
    docs, width = d.shape
    order = list(range(0, n, 2)) + list(range(n - 1, 0, -2))

    def turn(k):
        return [(order[p], order[(p + k) % n]) for p in range(n)]

    me = lax.axis_index("feat")
    pos = jnp.where(me % 2 == 0, me // 2, n - 1 - me // 2)

    def owner(k):
        p = (pos + k + n) % n
        return jnp.where(p < n // 2, 2 * p, 2 * (n - 1 - p) + 1)

    def rows(k, first, count):
        return lax.dynamic_slice(m, (owner(k) * width + first, 0), (count, m.shape[1]))

    q_all = gather_rows(q, "corp", n_corp)
    up = down = d
    applied = dot(d, rows(0, 0, width))
    half = width // 2
    for s in range(1, n // 2 + 1):
        if s < n // 2:
            up = lax.ppermute(up, "feat", turn(1))
            down = lax.ppermute(down, "feat", turn(-1))
            applied = applied + dot(up, rows(-s, 0, width))
            applied = applied + dot(down, rows(s, 0, width))
        else:
            up = lax.ppermute(up[:, :half], "feat", turn(1))
            down = lax.ppermute(down[:, half:], "feat", turn(-1))
            applied = applied + dot(up, rows(-s, 0, half))
            applied = applied + dot(down, rows(s, half, half))
    both = dot_t(q_all, jnp.concatenate(split(applied), 0))
    scores = both[:, :docs] + both[:, docs:]
    return scatter_sum(scores.reshape(n, -1, docs), n)


def plain_body(q, m, d):
    applied = dot(lax.all_gather(d, "feat", axis=1, tiled=True), m)
    left = lax.all_gather(q, "corp", axis=0, tiled=True).astype(F32)
    scores = lax.dot_general(
        left, applied, (((1,), (1,)), ((), ())), precision=lax.Precision.HIGHEST, preferred_element_type=F32
    )
    return lax.psum_scatter(scores, "feat", scatter_dimension=0, tiled=True)


def solution(mesh):
    n, n_corp = mesh.shape["feat"], mesh.shape["corp"]

    def on_device(q, m, d):
        if n % 4 == 0 and n <= 16:
            return ring_body(n, n_corp, q, m, d)
        return plain_body(q, m, d)

    placed = (P(("groups", "corp"), "feat"), P(None, "feat"), P(("groups", "corp"), "feat"))
    return jax.shard_map(
        on_device,
        mesh=mesh,
        in_specs=placed,
        out_specs=P(("groups", "feat"), "corp"),
        check_vma=False,
    )
```

```python
import functools

import jax
import jax.numpy as jnp
from jax import lax
from jax.experimental import pallas as pl
from jax.experimental.pallas import tpu as pltpu
from jax.sharding import PartitionSpec as P


F32 = jnp.float32
BF16 = jnp.bfloat16
SLOTS = 4
TILE_BYTES = 2 << 20


def dot(a, b):
    return jnp.dot(a, b, preferred_element_type=F32)


def dot_t(a, b):
    return lax.dot_general(a, b, (((1,), (1,)), ((), ())), preferred_element_type=F32)


def stream(row_ref, blocks, m_ref, tiles, sems, acc_ref):
    depth = tiles.shape[1]
    counts = [b.shape[1] // depth for b in blocks]
    total = sum(counts)

    def copy(i, start):
        slot = lax.rem(i, SLOTS)
        rows = pl.ds(pl.multiple_of(start, depth), depth)
        return pltpu.make_async_copy(m_ref.at[rows, :], tiles.at[slot], sems.at[slot])

    def start_of(i):
        row = row_ref[0] + i * depth
        base = counts[0]
        for b in range(1, len(blocks)):
            row = jnp.where(i >= base, row_ref[b] + (i - base) * depth, row)
            base += counts[b]
        return row

    for i in range(min(SLOTS, total)):
        copy(i, start_of(i)).start()
    first = 0
    for block, count in zip(blocks, counts):

        def step(j, carry, block=block, first=first):
            i = first + j
            copy(i, 0).wait()
            piece = block[:, pl.ds(pl.multiple_of(j * depth, depth), depth)]
            acc_ref[...] += dot(piece, tiles[lax.rem(i, SLOTS)])

            @pl.when(i + SLOTS < total)
            def _():
                copy(i + SLOTS, start_of(i + SLOTS)).start()

            return carry

        lax.fori_loop(0, count, step, 0)
        first += count


def apply_kernel(n_blocks, has_acc, row_ref, *refs):
    blocks, refs = refs[:n_blocks], refs[n_blocks:]
    m_ref, refs = refs[0], refs[1:]
    if has_acc:
        in_ref, refs = refs[0], refs[1:]
    out_ref, tiles, sems = refs
    out_ref[...] = in_ref[...] if has_acc else jnp.zeros_like(out_ref)
    stream(row_ref, blocks, m_ref, tiles, sems, out_ref)


def score_kernel(n_blocks, n_parts, row_ref, *refs):
    blocks, refs = refs[:n_blocks], refs[n_blocks:]
    m_ref, in_ref, refs = refs[0], refs[1], refs[2:]
    q_refs, (out_ref, acc, tiles, sems) = refs[:n_parts], refs[n_parts:]
    acc[...] = in_ref[...]
    stream(row_ref, blocks, m_ref, tiles, sems, acc)
    hi = acc[...].astype(BF16)
    lo = (acc[...] - hi.astype(F32)).astype(BF16)
    rows = q_refs[0].shape[0]
    for k, q_ref in enumerate(q_refs):
        at = pl.multiple_of(row_ref[n_blocks + k] * rows, rows)
        out_ref[pl.ds(at, rows), :] = dot_t(q_ref[...], hi) + dot_t(q_ref[...], lo)


def tile_depth(m, blocks):
    depth = TILE_BYTES // (m.shape[1] * m.dtype.itemsize)
    return min(depth, *(b.shape[1] for b in blocks))


def call(kernel, rows, operands, specs, out_shape, m, blocks, scratch, extra_flops=0):
    depth = tile_depth(m, blocks)
    width = sum(b.shape[1] for b in blocks)
    vmem = pl.BlockSpec(memory_space=pltpu.VMEM)
    return pl.pallas_call(
        kernel,
        out_shape=out_shape,
        in_specs=[pl.BlockSpec(memory_space=pltpu.SMEM)] + specs,
        out_specs=vmem,
        scratch_shapes=scratch
        + [pltpu.VMEM((SLOTS, depth, m.shape[1]), BF16), pltpu.SemaphoreType.DMA((SLOTS,))],
        cost_estimate=pl.CostEstimate(
            flops=2 * blocks[0].shape[0] * width * m.shape[1] + extra_flops,
            bytes_accessed=2 * width * m.shape[1],
            transcendentals=0,
        ),
        compiler_params=pltpu.CompilerParams(vmem_limit_bytes=32 << 20),
    )(rows, *operands)


VMEM = pl.BlockSpec(memory_space=pltpu.VMEM)
ANY = pl.BlockSpec(memory_space=pl.ANY)


def apply(acc, blocks, rows, m):
    shape = jax.ShapeDtypeStruct((blocks[0].shape[0], m.shape[1]), F32)
    operands = list(blocks) + [m] + ([] if acc is None else [acc])
    specs = [VMEM] * len(blocks) + [ANY] + ([] if acc is None else [VMEM])
    kernel = functools.partial(apply_kernel, len(blocks), acc is not None)
    return call(kernel, jnp.stack(rows), operands, specs, shape, m, blocks, [])


def score(acc, blocks, rows, m, parts, places):
    docs = blocks[0].shape[0]
    queries = sum(p.shape[0] for p in parts)
    shape = jax.ShapeDtypeStruct((queries, docs), F32)
    operands = list(blocks) + [m, acc] + parts
    specs = [VMEM] * len(blocks) + [ANY, VMEM] + [VMEM] * len(parts)
    kernel = functools.partial(score_kernel, len(blocks), len(parts))
    scratch = [pltpu.VMEM(acc.shape, F32)]
    flops = 4 * queries * docs * m.shape[1]
    return call(kernel, jnp.stack(rows + places), operands, specs, shape, m, blocks, scratch, flops)


def scatter_sum(s, n):
    me = lax.axis_index("feat")
    x, z, m = lax.rem(me, 2), lax.div(me, 2), n // 2
    s = s.reshape((m, 2) + s.shape[1:])
    mine = lax.dynamic_index_in_dim(s, x, 1, False)
    theirs = lax.dynamic_index_in_dim(s, 1 - x, 1, False)
    s = mine + lax.ppermute(theirs, "feat", [(i, i ^ 1) for i in range(n)])
    out = lax.dynamic_index_in_dim(s, z, 0, False)
    for k in range(1, m):
        y = lax.dynamic_index_in_dim(s, lax.rem(z + k, m), 0, False)
        out = out + lax.ppermute(y, "feat", [(i, (i + 2 * k) % n) for i in range(n)])
    return out


def ring_body(n, n_corp, q, m, d):
    docs, width = d.shape
    half = width // 2
    far = n // 2
    order = list(range(0, n, 2)) + list(range(n - 1, 0, -2))

    def turn(x, k):
        return lax.ppermute(x, "feat", [(order[p], order[(p + k) % n]) for p in range(n)])

    table = [[order[(order.index(f) + k) % n] * width for k in range(n)] for f in range(n)]
    starts = jnp.array(table, jnp.int32)[lax.axis_index("feat")]

    def at(k):
        return starts[k % n]

    core = lax.axis_index("corp")
    up, down = turn(d, 1), turn(d, -1)
    parts = [q] + [
        lax.ppermute(q, "corp", [(i, (i + k) % n_corp) for i in range(n_corp)]) for k in range(1, n_corp)
    ]
    places = [lax.rem(core + n_corp - k, n_corp) for k in range(n_corp)]
    acc = apply(None, [d], [at(0)], m)
    for s in range(1, far - 1):
        if s < far - 2:
            new_up, new_down = turn(up, 1), turn(down, -1)
        else:
            up_a, down_a = turn(up[:, :half], 1), turn(down[:, half:], -1)
            up_b, down_b = turn(up[:, half:], 1), turn(down[:, :half], -1)
        acc = apply(acc, [up, down], [at(-s), at(s)], m)
        if s < far - 2:
            up, down = new_up, new_down
    s = far - 1
    up_z, down_z = turn(up_a, 1), turn(down_a, -1)
    acc = apply(acc, [up_a, down_a], [at(-s), at(s) + half], m)
    acc = apply(acc, [up_b, down_b], [at(-s) + half, at(s)], m)
    scores = score(acc, [up_z, down_z], [at(far), at(far) + half], m, parts, places)
    return scatter_sum(scores.reshape(n, -1, docs), n)


def plain_body(q, m, d):
    applied = dot(lax.all_gather(d, "feat", axis=1, tiled=True), m)
    left = lax.all_gather(q, "corp", axis=0, tiled=True).astype(F32)
    scores = lax.dot_general(
        left, applied, (((1,), (1,)), ((), ())), precision=lax.Precision.HIGHEST, preferred_element_type=F32
    )
    return lax.psum_scatter(scores, "feat", scatter_dimension=0, tiled=True)


def solution(mesh):
    n, n_corp = mesh.shape["feat"], mesh.shape["corp"]
    ring = n % 4 == 0 and 8 <= n <= 16

    def on_device(q, m, d):
        if not ring:
            return plain_body(q, m, d)
        return ring_body(n, n_corp, q, m, d)

    placed = (P(("groups", "corp"), "feat"), P(None, "feat"), P(("groups", "corp"), "feat"))
    return jax.shard_map(
        on_device,
        mesh=mesh,
        in_specs=placed,
        out_specs=P(("groups", "feat"), "corp"),
        check_vma=False,
    )
```

```python
import functools

import jax
import jax.numpy as jnp
from jax import lax
from jax.experimental import pallas as pl
from jax.experimental.pallas import tpu as pltpu
from jax.sharding import PartitionSpec as P


F32 = jnp.float32
BF16 = jnp.bfloat16
SLOTS = 6
TILE_ROWS = 512


def dot(a, b):
    return jnp.dot(a, b, preferred_element_type=F32)


def dot_t(a, b):
    return lax.dot_general(a, b, (((1,), (1,)), ((), ())), preferred_element_type=F32)


def ring_order(n):
    return list(range(0, n, 2)) + list(range(n - 1, 0, -2))


def ring_owner(n, k):
    me = lax.axis_index("feat")
    place = jnp.where(lax.rem(me, 2) == 0, lax.div(me, 2), n - 1 - lax.div(me, 2))
    place = lax.rem(place + (k + n) % n, n)
    return jnp.where(place < n // 2, 2 * place, 2 * (n - 1 - place) + 1)


def stream(n, rows, blocks, m_ref, tiles, sems, acc_ref):
    slots, depth, width = tiles.shape
    counts = [b.shape[1] // depth for b in blocks]
    total = sum(counts)
    starts = [ring_owner(n, k) * width + first for k, first in rows]

    def copy(i, start):
        slot = lax.rem(i, slots)
        at = pl.ds(pl.multiple_of(start, depth), depth)
        return pltpu.make_async_copy(m_ref.at[at, :], tiles.at[slot], sems.at[slot])

    def start_of(i):
        row, base = starts[0] + i * depth, counts[0]
        for b in range(1, len(blocks)):
            row = jnp.where(i >= base, starts[b] + (i - base) * depth, row)
            base += counts[b]
        return row

    for i in range(min(slots, total)):
        copy(i, start_of(i)).start()
    first = 0
    for block, count in zip(blocks, counts):

        def step(j, carry, block=block, first=first):
            i = first + j
            copy(i, 0).wait()
            piece = block[:, pl.ds(pl.multiple_of(j * depth, depth), depth)]
            acc_ref[...] += dot(piece, tiles[lax.rem(i, slots)])

            @pl.when(i + slots < total)
            def _():
                copy(i + slots, start_of(i + slots)).start()

            return carry

        lax.fori_loop(0, count, step, 0)
        first += count


def apply_kernel(n, rows, has_acc, *refs):
    blocks, refs = refs[: len(rows)], refs[len(rows) :]
    m_ref, out_ref, tiles, sems = refs[0], refs[-3], refs[-2], refs[-1]
    if not has_acc:
        out_ref[...] = jnp.zeros_like(out_ref)
    stream(n, rows, blocks, m_ref, tiles, sems, out_ref)


def score_kernel(n, rows, n_parts, *refs):
    blocks, refs = refs[: len(rows)], refs[len(rows) :]
    m_ref, in_ref, refs = refs[0], refs[1], refs[2:]
    q_refs, (out_ref, acc, pair, tiles, sems) = refs[:n_parts], refs[n_parts:]
    acc[...] = in_ref[...]
    stream(n, rows, blocks, m_ref, tiles, sems, acc)
    docs = acc.shape[0]
    hi = acc[...].astype(BF16)
    pair[:docs, :] = hi
    pair[docs:, :] = (acc[...] - hi.astype(F32)).astype(BF16)
    count = q_refs[0].shape[0]
    for k, q_ref in enumerate(q_refs):
        place = lax.rem(lax.axis_index("corp") + n_parts - k, n_parts)
        both = dot_t(q_ref[...], pair[...])
        out_ref[pl.ds(pl.multiple_of(place * count, count), count), :] = both[:, :docs] + both[:, docs:]


def call(kernel, operands, out_shape, m, blocks, scratch, extra_flops=0, aliases=None):
    depth = min(TILE_ROWS, *(b.shape[1] for b in blocks))
    width = sum(b.shape[1] for b in blocks)
    return pl.pallas_call(
        kernel,
        out_shape=out_shape,
        in_specs=[pl.BlockSpec(memory_space=pl.ANY if x is m else pltpu.VMEM) for x in operands],
        out_specs=pl.BlockSpec(memory_space=pltpu.VMEM),
        scratch_shapes=scratch
        + [pltpu.VMEM((SLOTS, depth, m.shape[1]), BF16), pltpu.SemaphoreType.DMA((SLOTS,))],
        input_output_aliases=aliases or {},
        cost_estimate=pl.CostEstimate(
            flops=2 * blocks[0].shape[0] * width * m.shape[1] + extra_flops,
            bytes_accessed=2 * width * m.shape[1],
            transcendentals=0,
        ),
        compiler_params=pltpu.CompilerParams(vmem_limit_bytes=32 << 20),
    )(*operands)


def apply(n, acc, blocks, rows, m):
    shape = jax.ShapeDtypeStruct((blocks[0].shape[0], m.shape[1]), F32)
    operands = list(blocks) + [m] + ([] if acc is None else [acc])
    kernel = functools.partial(apply_kernel, n, rows, acc is not None)
    return call(kernel, operands, shape, m, blocks, [], aliases=None if acc is None else {len(blocks) + 1: 0})


def score(n, acc, blocks, rows, m, parts):
    docs = blocks[0].shape[0]
    queries = sum(p.shape[0] for p in parts)
    shape = jax.ShapeDtypeStruct((queries, docs), F32)
    kernel = functools.partial(score_kernel, n, rows, len(parts))
    scratch = [pltpu.VMEM(acc.shape, F32), pltpu.VMEM((2 * docs, m.shape[1]), BF16)]
    flops = 4 * queries * docs * m.shape[1]
    return call(kernel, list(blocks) + [m, acc] + parts, shape, m, blocks, scratch, flops)


def scatter_sum(s, n):
    me = lax.axis_index("feat")
    x, z, m = lax.rem(me, 2), lax.div(me, 2), n // 2
    s = s.reshape((m, 2) + s.shape[1:])
    mine = lax.dynamic_index_in_dim(s, x, 1, False)
    theirs = lax.dynamic_index_in_dim(s, 1 - x, 1, False)
    s = mine + lax.ppermute(theirs, "feat", [(i, i ^ 1) for i in range(n)])
    out = lax.dynamic_index_in_dim(s, z, 0, False)
    for k in range(1, m):
        y = lax.dynamic_index_in_dim(s, lax.rem(z + k, m), 0, False)
        out = out + lax.ppermute(y, "feat", [(i, (i + 2 * k) % n) for i in range(n)])
    return out


def ring_body(n, n_corp, q, m, d):
    docs, width = d.shape
    half = width // 2
    far = n // 2
    order = ring_order(n)

    def turn(x, k):
        return lax.ppermute(x, "feat", [(order[p], order[(p + k) % n]) for p in range(n)])

    def run(*args):
        return apply(n, *args, m)

    up, down = turn(d, 1), turn(d, -1)
    parts = [q] + [lax.ppermute(q, "corp", [(i, (i + k) % n_corp) for i in range(n_corp)]) for k in range(1, n_corp)]
    acc = run(None, [d], [(0, 0)])
    for s in range(1, far - 1):
        if s < far - 2:
            new_up, new_down = turn(up, 1), turn(down, -1)
        else:
            up_a, down_a = turn(up[:, :half], 1), turn(down[:, half:], -1)
            up_b, down_b = turn(up[:, half:], 1), turn(down[:, :half], -1)
        acc = run(acc, [up, down], [(-s, 0), (s, 0)])
        if s < far - 2:
            up, down = new_up, new_down
    s = far - 1
    up_z, down_z = turn(up_a, 1), turn(down_a, -1)
    acc = run(acc, [up_a, down_a, up_b, down_b], [(-s, 0), (s, half), (-s, half), (s, 0)])
    scores = score(n, acc, [up_z, down_z], [(far, 0), (far, half)], m, parts)
    return scatter_sum(scores.reshape(n, -1, docs), n)


def plain_body(q, m, d):
    applied = dot(lax.all_gather(d, "feat", axis=1, tiled=True), m)
    left = lax.all_gather(q, "corp", axis=0, tiled=True).astype(F32)
    scores = lax.dot_general(
        left, applied, (((1,), (1,)), ((), ())), precision=lax.Precision.HIGHEST, preferred_element_type=F32
    )
    return lax.psum_scatter(scores, "feat", scatter_dimension=0, tiled=True)


def solution(mesh):
    n, n_corp = mesh.shape["feat"], mesh.shape["corp"]
    ring = n % 4 == 0 and 8 <= n <= 16

    def on_device(q, m, d):
        if not ring:
            return plain_body(q, m, d)
        return ring_body(n, n_corp, q, m, d)

    placed = (P(("groups", "corp"), "feat"), P(None, "feat"), P(("groups", "corp"), "feat"))
    return jax.shard_map(
        on_device,
        mesh=mesh,
        in_specs=placed,
        out_specs=P(("groups", "feat"), "corp"),
        check_vma=False,
    )
```

```python
import functools

import jax
import jax.numpy as jnp
from jax import lax
from jax.experimental import pallas as pl
from jax.experimental.pallas import tpu as pltpu
from jax.sharding import PartitionSpec as P


F32 = jnp.float32
BF16 = jnp.bfloat16
SLOTS = 5
TILE_ROWS = 512


def dot(a, b):
    return jnp.dot(a, b, preferred_element_type=F32)


def dot_t(a, b):
    return lax.dot_general(a, b, (((1,), (1,)), ((), ())), preferred_element_type=F32)


def ring_order(n):
    return list(range(0, n, 2)) + list(range(n - 1, 0, -2))


def ring_owner(n, k):
    me = lax.axis_index("feat")
    place = jnp.where(lax.rem(me, 2) == 0, lax.div(me, 2), n - 1 - lax.div(me, 2))
    place = lax.rem(place + k, n)
    return jnp.where(place < n // 2, 2 * place, 2 * (n - 1 - place) + 1)


def stream(n, rows, blocks, loads, m_ref, tiles, sems, acc_refs):
    slots, depth, width = tiles.shape
    counts = [b[0].shape[1] // depth for b in blocks]
    total = sum(counts)
    core = lax.axis_index("corp")
    half = width // 2
    starts = [
        ring_owner(n, jnp.where(core == 0, k, n - k)) * width + (1 - core if flip else core) * half for k, flip in rows
    ]

    def copy(i, start):
        slot = lax.rem(i, slots)
        at = pl.ds(pl.multiple_of(start, depth), depth)
        return pltpu.make_async_copy(m_ref.at[at, :], tiles.at[slot], sems.at[slot])

    def start_of(i):
        row, base = starts[0] + i * depth, counts[0]
        for b in range(1, len(blocks)):
            row = jnp.where(i >= base, starts[b] + (i - base) * depth, row)
            base += counts[b]
        return row

    for i in range(min(slots, total)):
        copy(i, start_of(i)).start()
    first = 0
    for block, count in zip(blocks, counts):
        for load in loads[: len(block)]:
            load.wait()
        loads = loads[len(block) :]

        def step(j, carry, block=block, first=first):
            i = first + j
            copy(i, 0).wait()
            at = pl.ds(pl.multiple_of(j * depth, depth), depth)
            piece = jnp.concatenate([ref[:, at] for ref in block], 0)
            product = dot(piece, tiles[lax.rem(i, slots)])
            docs = block[0].shape[0]
            for k, acc_ref in enumerate(acc_refs):
                acc_ref[...] += product[k * docs : (k + 1) * docs]

            @pl.when(i + slots < total)
            def _():
                copy(i + slots, start_of(i + slots)).start()

            return carry

        lax.fori_loop(0, count, step, 0)
        first += count


def apply_kernel(n, rows, sets, has_acc, *refs):
    count = sets * len(rows)
    m_ref, out_refs, (pieces, piece_sems, tiles, sems) = refs[count], refs[-4 - sets : -4], refs[-4:]
    loads = [pltpu.make_async_copy(refs[i], pieces.at[i], piece_sems.at[i]) for i in range(count)]
    for load in loads:
        load.start()
    if not has_acc:
        for out_ref in out_refs:
            out_ref[...] = jnp.zeros_like(out_ref)
    blocks = [[pieces.at[b * sets + k] for k in range(sets)] for b in range(len(rows))]
    stream(n, rows, blocks, loads, m_ref, tiles, sems, out_refs)


def apply(n, accs, blocks, rows, m):
    pieces = [p for b in blocks for p in b]
    sets = len(blocks[0])
    docs, span = pieces[0].shape
    depth = min(TILE_ROWS, span)
    any_spec = pl.BlockSpec(memory_space=pl.ANY)
    vmem = pl.BlockSpec(memory_space=pltpu.VMEM)
    return pl.pallas_call(
        functools.partial(apply_kernel, n, rows, sets, bool(accs)),
        out_shape=[jax.ShapeDtypeStruct((docs, m.shape[1]), F32)] * sets,
        in_specs=[any_spec] * (len(pieces) + 1) + [vmem] * len(accs),
        out_specs=[vmem] * sets,
        scratch_shapes=[
            pltpu.VMEM((len(pieces), docs, span), BF16),
            pltpu.SemaphoreType.DMA((len(pieces),)),
            pltpu.VMEM((SLOTS, depth, m.shape[1]), BF16),
            pltpu.SemaphoreType.DMA((SLOTS,)),
        ],
        input_output_aliases={len(pieces) + 1 + k: k for k in range(len(accs))},
        cost_estimate=pl.CostEstimate(
            flops=2 * docs * len(pieces) * span * m.shape[1],
            bytes_accessed=2 * len(blocks) * span * m.shape[1],
            transcendentals=0,
        ),
        compiler_params=pltpu.CompilerParams(vmem_limit_bytes=24 << 20),
    )(*pieces, m, *accs)


def score_kernel(*refs):
    first_ref, second_ref, *q_refs, out_ref, pair = refs
    docs = first_ref.shape[0]
    total = first_ref[...] + second_ref[...]
    hi = total.astype(BF16)
    pair[:docs, :] = hi
    pair[docs:, :] = (total - hi.astype(F32)).astype(BF16)
    height = q_refs[0].shape[0]
    for k, q_ref in enumerate(q_refs):
        place = lax.rem(lax.axis_index("corp") + len(q_refs) - k, len(q_refs))
        both = dot_t(q_ref[...], pair[...])
        out_ref[pl.ds(pl.multiple_of(place * height, height), height), :] = both[:, :docs] + both[:, docs:]


def score(first, second, parts):
    queries = sum(p.shape[0] for p in parts)
    docs, width = first.shape
    vmem = pl.BlockSpec(memory_space=pltpu.VMEM)
    return pl.pallas_call(
        score_kernel,
        out_shape=jax.ShapeDtypeStruct((queries, docs), F32),
        in_specs=[vmem] * (2 + len(parts)),
        out_specs=vmem,
        scratch_shapes=[pltpu.VMEM((2 * docs, width), BF16)],
        cost_estimate=pl.CostEstimate(
            flops=4 * queries * docs * width, bytes_accessed=2 * queries * width, transcendentals=0
        ),
        compiler_params=pltpu.CompilerParams(vmem_limit_bytes=16 << 20),
    )(first, second, *parts)


def scatter_sum(s, n):
    me = lax.axis_index("feat")
    x, z, m = lax.rem(me, 2), lax.div(me, 2), n // 2
    s = s.reshape((m, 2) + s.shape[1:])
    mine = lax.dynamic_index_in_dim(s, x, 1, False)
    theirs = lax.dynamic_index_in_dim(s, 1 - x, 1, False)
    s = mine + lax.ppermute(theirs, "feat", [(i, i ^ 1) for i in range(n)])
    out = lax.dynamic_index_in_dim(s, z, 0, False)
    for k in range(1, m):
        y = lax.dynamic_index_in_dim(s, lax.rem(z + k, m), 0, False)
        out = out + lax.ppermute(y, "feat", [(i, (i + 2 * k) % n) for i in range(n)])
    return out


def ring_body(n, q, m, d):
    docs, width = d.shape
    half = width // 2
    far = n // 2
    order = ring_order(n)
    core = lax.axis_index("corp")

    def move(x, shift, cross):
        pairs = [
            (2 * order[p] + c, 2 * order[(p + shift(c)) % n] + (c ^ cross)) for p in range(n) for c in range(2)
        ]
        return lax.ppermute(x, ("feat", "corp"), pairs)

    def fore(c):
        return 1 - 2 * c

    def back(c):
        return 2 * c - 1

    p_fore = p_back = lax.dynamic_slice(d, (0, core * half), (docs, half))
    r_fore = r_back = lax.dynamic_slice(d, (0, (1 - core) * half), (docs, half))
    own_p = p_fore
    own_r = move(r_fore, lambda c: 0, 1)
    parts = [q, lax.ppermute(q, "corp", [(0, 1), (1, 0)])]
    accs = []
    blocks, rows = [(own_p, own_r)], [(0, False)]
    for s in range(1, far):
        r_ways = (back, fore) if s == 1 else (fore, back)
        p_fore, p_back = move(p_fore, fore, 0), move(p_back, back, 0)
        r_fore = move(r_fore, r_ways[0], s == 1)
        r_back = move(r_back, r_ways[1], s == 1)
        accs = apply(n, accs, blocks, rows, m)
        blocks, rows = [(p_fore, r_fore), (p_back, r_back)], [(n - s, False), (s, False)]

    z_p, z_r = move(p_fore, fore, 0), move(r_fore, fore, 1)
    mine, theirs = apply(n, accs, blocks, rows, m)
    other = lax.ppermute(theirs, "corp", [(0, 1), (1, 0)])
    (mine,) = apply(n, [mine], [(z_p,), (z_r,)], [(far, False), (far, True)], m)
    scores = score(mine, other, parts)
    return scatter_sum(scores.reshape(n, -1, docs), n)


def plain_body(q, m, d):
    applied = dot(lax.all_gather(d, "feat", axis=1, tiled=True), m)
    left = lax.all_gather(q, "corp", axis=0, tiled=True).astype(F32)
    scores = lax.dot_general(
        left, applied, (((1,), (1,)), ((), ())), precision=lax.Precision.HIGHEST, preferred_element_type=F32
    )
    return lax.psum_scatter(scores, "feat", scatter_dimension=0, tiled=True)


def solution(mesh):
    n, n_corp = mesh.shape["feat"], mesh.shape["corp"]
    ring = n % 4 == 0 and 8 <= n <= 16 and n_corp == 2

    def on_device(q, m, d):
        if not ring:
            return plain_body(q, m, d)
        return ring_body(n, q, m, d)

    placed = (P(("groups", "corp"), "feat"), P(None, "feat"), P(("groups", "corp"), "feat"))
    return jax.shard_map(
        on_device,
        mesh=mesh,
        in_specs=placed,
        out_specs=P(("groups", "feat"), "corp"),
        check_vma=False,
    )
```

```python
import functools

import jax
import jax.numpy as jnp
from jax import lax
from jax.experimental import pallas as pl
from jax.experimental.pallas import tpu as pltpu
from jax.sharding import PartitionSpec as P


F32 = jnp.float32
BF16 = jnp.bfloat16
SLOTS = 5
TILE_ROWS = 512
KEPT_ROWS = 1024


def dot(a, b):
    return jnp.dot(a, b, preferred_element_type=F32)


def dot_t(a, b):
    return lax.dot_general(a, b, (((1,), (1,)), ((), ())), preferred_element_type=F32)


def ring_order(n):
    return list(range(0, n, 2)) + list(range(n - 1, 0, -2))


def ring_owner(n, k):
    me = lax.axis_index("feat")
    place = jnp.where(lax.rem(me, 2) == 0, lax.div(me, 2), n - 1 - lax.div(me, 2))
    place = lax.rem(place + k, n)
    return jnp.where(place < n // 2, 2 * place, 2 * (n - 1 - place) + 1)


def row_starts(n, rows, width):
    core = lax.axis_index("corp")
    half = width // 2
    return [
        ring_owner(n, jnp.where(core == 0, k, n - k)) * width + (1 - core if flip else core) * half for k, flip in rows
    ]


def stream(n, rows, blocks, loads, m_ref, tiles, sems, acc_refs, behind=()):
    slots, depth, width = tiles.shape
    counts = [b[0].shape[1] // depth for b in blocks]
    total = sum(counts)
    starts = row_starts(n, rows, width)

    def copy(i, start):
        slot = lax.rem(i, slots)
        at = pl.ds(pl.multiple_of(start, depth), depth)
        return pltpu.make_async_copy(m_ref.at[at, :], tiles.at[slot], sems.at[slot])

    def start_of(i):
        row, base = starts[0] + i * depth, counts[0]
        for b in range(1, len(blocks)):
            row = jnp.where(i >= base, starts[b] + (i - base) * depth, row)
            base += counts[b]
        return row

    for i in range(min(slots, total)):
        copy(i, start_of(i)).start()
    for other in behind:
        other.start()
    first = 0
    for block, count in zip(blocks, counts):
        for load in loads[: len(block)]:
            load.wait()
        loads = loads[len(block) :]

        def step(j, carry, block=block, first=first):
            i = first + j
            copy(i, 0).wait()
            at = pl.ds(pl.multiple_of(j * depth, depth), depth)
            piece = jnp.concatenate([ref[:, at] for ref in block], 0)
            product = dot(piece, tiles[lax.rem(i, slots)])
            docs = block[0].shape[0]
            for k, acc_ref in enumerate(acc_refs):
                acc_ref[...] += product[k * docs : (k + 1) * docs]

            @pl.when(i + slots < total)
            def _():
                copy(i + slots, start_of(i + slots)).start()

            return carry

        lax.fori_loop(0, count, step, 0)
        first += count


def load_pieces(sources, pieces, sems):
    loads = [pltpu.make_async_copy(ref, pieces.at[i], sems.at[i]) for i, ref in enumerate(sources)]
    for load in loads:
        load.start()
    return loads


def apply_kernel(n, rows, sets, n_kept, keep, *refs):
    count = sets * len(rows)
    m_ref, outs, (pieces, piece_sems, tiles, sems, keep_sems) = refs[count], refs[-5 - sets - n_kept : -5], refs[-5:]
    out_refs, kept = outs[:sets], outs[sets:]
    loads = load_pieces(refs[:count], pieces, piece_sems)
    copies = []
    if keep:
        for out_ref in out_refs:
            out_ref[...] = jnp.zeros_like(out_ref)
        height = kept[0].shape[0]
        starts = row_starts(n, keep, m_ref.shape[1])
        for i in range(n_kept):
            first, part = divmod(i * len(keep), n_kept)
            row = starts[first] + part // len(keep) * height
            at = pl.ds(pl.multiple_of(row, height), height)
            copies.append(pltpu.make_async_copy(m_ref.at[at, :], kept[i], keep_sems.at[i]))
    blocks = [[pieces.at[b * sets + k] for k in range(sets)] for b in range(len(rows))]
    stream(n, rows, blocks, loads, m_ref, tiles, sems, out_refs, copies)
    for copy in copies:
        copy.wait()


def score_kernel(n_pieces, n_kept, n_parts, *refs):
    in_ref, other_ref, *kept = refs[n_pieces : n_pieces + 2 + n_kept]
    q_refs, (out_ref, acc, pair, queries, q_sems, pieces, piece_sems) = refs[n_pieces + 2 + n_kept : -7], refs[-7:]
    loads = load_pieces(refs[:n_pieces], pieces, piece_sems)
    q_loads = load_pieces(q_refs, queries, q_sems)
    acc[...] = in_ref[...] + other_ref[...]
    each, depth = n_kept // n_pieces, kept[0].shape[0]
    for i in range(n_pieces):
        loads[i].wait()
        for j in range(each):
            acc[...] += dot(pieces[i, :, j * depth : (j + 1) * depth], kept[i * each + j][...])
    docs = acc.shape[0]
    hi = acc[...].astype(BF16)
    pair[:docs, :] = hi
    pair[docs:, :] = (acc[...] - hi.astype(F32)).astype(BF16)
    height = queries.shape[1]
    for k in range(n_parts):
        q_loads[k].wait()
        place = lax.rem(lax.axis_index("corp") + n_parts - k, n_parts)
        both = dot_t(queries[k], pair[...])
        out_ref[pl.ds(pl.multiple_of(place * height, height), height), :] = both[:, :docs] + both[:, docs:]


VMEM = pl.BlockSpec(memory_space=pltpu.VMEM)
ANY = pl.BlockSpec(memory_space=pl.ANY)


def call(kernel, out_shape, operands, specs, scratch, flops, n_bytes, aliases):
    return pl.pallas_call(
        kernel,
        out_shape=out_shape,
        in_specs=specs,
        out_specs=jax.tree.map(lambda _: VMEM, out_shape),
        scratch_shapes=scratch,
        input_output_aliases=aliases,
        cost_estimate=pl.CostEstimate(flops=flops, bytes_accessed=n_bytes, transcendentals=0),
        compiler_params=pltpu.CompilerParams(vmem_limit_bytes=24 << 20),
    )(*operands)


def piece_scratch(pieces):
    return [pltpu.VMEM((len(pieces),) + pieces[0].shape, BF16), pltpu.SemaphoreType.DMA((len(pieces),))]


def apply(n, accs, kept, blocks, rows, m, keep=()):
    pieces = [p for b in blocks for p in b]
    sets = len(blocks[0])
    docs, span = pieces[0].shape
    depth = min(TILE_ROWS, span)
    n_kept = len(keep) * span // KEPT_ROWS if keep else len(kept)
    shape = [jax.ShapeDtypeStruct((docs, m.shape[1]), F32)] * sets
    shape += [jax.ShapeDtypeStruct((KEPT_ROWS, m.shape[1]), BF16)] * n_kept
    carried = [] if keep else accs + kept
    scratch = piece_scratch(pieces) + [
        pltpu.VMEM((SLOTS, depth, m.shape[1]), BF16),
        pltpu.SemaphoreType.DMA((SLOTS,)),
        pltpu.SemaphoreType.DMA((n_kept,)),
    ]
    outs = call(
        functools.partial(apply_kernel, n, rows, sets, n_kept, keep),
        shape,
        pieces + [m] + carried,
        [ANY] * (len(pieces) + 1) + [VMEM] * len(carried),
        scratch,
        2 * docs * len(pieces) * span * m.shape[1],
        2 * (len(rows) + len(keep)) * span * m.shape[1],
        {len(pieces) + 1 + k: k for k in range(len(carried))},
    )
    return list(outs[:sets]), list(outs[sets:])


def score(accs, kept, pieces, parts):
    queries = sum(p.shape[0] for p in parts)
    docs, width = accs[0].shape
    scratch = [
        pltpu.VMEM((docs, width), F32),
        pltpu.VMEM((2 * docs, width), BF16),
        *piece_scratch(parts),
        *piece_scratch(pieces),
    ]
    return call(
        functools.partial(score_kernel, len(pieces), len(kept), len(parts)),
        jax.ShapeDtypeStruct((queries, docs), F32),
        pieces + accs + kept + parts,
        [ANY] * len(pieces) + [VMEM] * (2 + len(kept)) + [ANY] * len(parts),
        scratch,
        2 * docs * width * (2 * queries + len(pieces) * pieces[0].shape[1]),
        2 * queries * width,
        {},
    )


def scatter_sum(s, n, me):
    x, z, m = lax.rem(me, 2), lax.div(me, 2), n // 2
    s = s.reshape((m, 2) + s.shape[1:])
    mine = lax.dynamic_index_in_dim(s, x, 1, False)
    theirs = lax.dynamic_index_in_dim(s, 1 - x, 1, False)
    s = mine + lax.ppermute(theirs, "feat", [(i, i ^ 1) for i in range(n)])
    out = lax.dynamic_index_in_dim(s, z, 0, False)
    for k in range(1, m):
        y = lax.dynamic_index_in_dim(s, lax.rem(z + k, m), 0, False)
        out = out + lax.ppermute(y, "feat", [(i, (i + 2 * k) % n) for i in range(n)])
    return out


def ring_body(n, q, m, d):
    docs, width = d.shape
    half = width // 2
    far = n // 2
    order = ring_order(n)
    d, me, core = lax.optimization_barrier((d, lax.axis_index("feat"), lax.axis_index("corp")))

    def move(x, shift, cross):
        pairs = [
            (2 * order[p] + c, 2 * order[(p + shift(c)) % n] + (c ^ cross)) for p in range(n) for c in range(2)
        ]
        return lax.ppermute(x, ("feat", "corp"), pairs)

    def fore(c):
        return 1 - 2 * c

    def back(c):
        return 2 * c - 1

    p_fore = p_back = lax.dynamic_slice(d, (0, core * half), (docs, half))
    r_fore = r_back = lax.dynamic_slice(d, (0, (1 - core) * half), (docs, half))
    own_p = p_fore
    own_r = move(r_fore, lambda c: 0, 1)
    parts = [q, lax.ppermute(q, "corp", [(0, 1), (1, 0)])]
    accs, kept = [], []
    blocks, rows = [(own_p, own_r)], [(0, False)]
    last_rows = [(far, False), (far, True)]
    for s in range(1, far):
        r_ways = (back, fore) if s == 1 else (fore, back)
        r_fore = move(r_fore, r_ways[0], s == 1)
        r_back = move(r_back, r_ways[1], s == 1)
        p_fore, p_back = move(p_fore, fore, 0), move(p_back, back, 0)
        accs, kept = apply(n, accs, kept, blocks, rows, m, last_rows if s == 1 else ())
        blocks, rows = [(p_fore, r_fore), (p_back, r_back)], [(n - s, False), (s, False)]

    mine, theirs = accs
    z_r, z_p = move(r_fore, fore, 1), move(p_fore, fore, 0)
    (theirs,), kept = apply(n, [theirs], kept, [(r_fore,), (r_back,)], rows, m)
    other = lax.ppermute(theirs, "corp", [(0, 1), (1, 0)])
    (mine,), kept = apply(n, [mine], kept, [(p_fore,), (p_back,)], rows, m)
    scores = score([mine, other], kept, [z_p, z_r], parts)
    scores, me = lax.optimization_barrier((scores, me))
    return scatter_sum(scores.reshape(n, -1, docs), n, me)


def plain_body(q, m, d):
    applied = dot(lax.all_gather(d, "feat", axis=1, tiled=True), m)
    left = lax.all_gather(q, "corp", axis=0, tiled=True).astype(F32)
    scores = lax.dot_general(
        left, applied, (((1,), (1,)), ((), ())), precision=lax.Precision.HIGHEST, preferred_element_type=F32
    )
    return lax.psum_scatter(scores, "feat", scatter_dimension=0, tiled=True)


def solution(mesh):
    n, n_corp = mesh.shape["feat"], mesh.shape["corp"]
    ring = n % 4 == 0 and 8 <= n <= 16 and n_corp == 2

    def on_device(q, m, d):
        if not ring:
            return plain_body(q, m, d)
        return ring_body(n, q, m, d)

    placed = (P(("groups", "corp"), "feat"), P(None, "feat"), P(("groups", "corp"), "feat"))
    return jax.shard_map(
        on_device,
        mesh=mesh,
        in_specs=placed,
        out_specs=P(("groups", "feat"), "corp"),
        check_vma=False,
    )
```

```python
import functools

import jax
import jax.numpy as jnp
from jax import lax
from jax.experimental import pallas as pl
from jax.experimental.pallas import tpu as pltpu
from jax.sharding import PartitionSpec as P


F32 = jnp.float32
BF16 = jnp.bfloat16
SLOTS = 3
TILE_ROWS = 1024


def dot(a, b):
    return jnp.dot(a, b, preferred_element_type=F32)


def dot_t(a, b):
    return lax.dot_general(a, b, (((1,), (1,)), ((), ())), preferred_element_type=F32)


def ring_order(n):
    return list(range(0, n, 2)) + list(range(n - 1, 0, -2))


def ring_owner(n, k):
    me = lax.axis_index("feat")
    place = jnp.where(lax.rem(me, 2) == 0, lax.div(me, 2), n - 1 - lax.div(me, 2))
    place = lax.rem(place + k, n)
    return jnp.where(place < n // 2, 2 * place, 2 * (n - 1 - place) + 1)


def row_starts(n, rows, width):
    core = lax.axis_index("corp")
    half = width // 2
    return [
        ring_owner(n, jnp.where(core == 0, k, n - k)) * width + (1 - core if flip else core) * half for k, flip in rows
    ]


def stream(n, rows, blocks, loads, m_ref, tiles, sems, acc_refs, behind=()):
    slots, depth, width = tiles.shape
    counts = [b[0].shape[1] // depth for b in blocks]
    total = sum(counts)
    starts = row_starts(n, rows, width)

    def copy(i, start):
        slot = lax.rem(i, slots)
        at = pl.ds(pl.multiple_of(start, depth), depth)
        return pltpu.make_async_copy(m_ref.at[at, :], tiles.at[slot], sems.at[slot])

    def start_of(i):
        row, base = starts[0] + i * depth, counts[0]
        for b in range(1, len(blocks)):
            row = jnp.where(i >= base, starts[b] + (i - base) * depth, row)
            base += counts[b]
        return row

    for i in range(min(slots, total)):
        copy(i, start_of(i)).start()
    for other in behind:
        other.start()
    first = 0
    for block, count in zip(blocks, counts):
        for load in loads[: len(block)]:
            load.wait()
        loads = loads[len(block) :]

        def step(j, carry, block=block, first=first):
            i = first + j
            copy(i, 0).wait()
            at = pl.ds(pl.multiple_of(j * depth, depth), depth)
            piece = jnp.concatenate([ref[:, at] for ref in block], 0)
            product = dot(piece, tiles[lax.rem(i, slots)])
            docs = block[0].shape[0]
            for k, acc_ref in enumerate(acc_refs):
                acc_ref[...] += product[k * docs : (k + 1) * docs]

            @pl.when(i + slots < total)
            def _():
                copy(i + slots, start_of(i + slots)).start()

            return carry

        lax.fori_loop(0, count, step, 0)
        first += count


def load_pieces(sources, pieces, sems):
    loads = [pltpu.make_async_copy(ref, pieces.at[i], sems.at[i]) for i, ref in enumerate(sources)]
    for load in loads:
        load.start()
    return loads


def apply_kernel(n, rows, sets, has_acc, n_kept, keep, *refs):
    count = sets * len(rows)
    n_out = sets + n_kept + len(keep)
    m_ref, outs, (pieces, piece_sems, tiles, sems, keep_sems) = refs[count], refs[-5 - n_out : -5], refs[-5:]
    out_refs, new = outs[:sets], outs[sets + n_kept :]
    loads = load_pieces(refs[:count], pieces, piece_sems)
    if not has_acc:
        for out_ref in out_refs:
            out_ref[...] = jnp.zeros_like(out_ref)
    copies = []
    for i, start in enumerate(row_starts(n, keep, m_ref.shape[1])):
        at = pl.ds(pl.multiple_of(start, new[i].shape[0]), new[i].shape[0])
        copies.append(pltpu.make_async_copy(m_ref.at[at, :], new[i], keep_sems.at[i]))
    blocks = [[pieces.at[b * sets + k] for k in range(sets)] for b in range(len(rows))]
    stream(n, rows, blocks, loads, m_ref, tiles, sems, out_refs, copies)
    for copy in copies:
        copy.wait()


def add_products(pieces, loads, kept, acc):
    for i, load in enumerate(loads):
        load.wait()
        acc[...] += dot(pieces[i], kept[i][...])


def add_kernel(n_pieces, *refs):
    kept, (out_ref, pieces, piece_sems) = refs[n_pieces : 2 * n_pieces], refs[-3:]
    add_products(pieces, load_pieces(refs[:n_pieces], pieces, piece_sems), kept, out_ref)


def score_kernel(n_pieces, n_parts, *refs):
    in_ref, other_ref, *kept = refs[n_pieces : 2 * n_pieces + 2]
    q_refs, (out_ref, acc, pair, queries, q_sems, pieces, piece_sems) = refs[2 * n_pieces + 2 : -7], refs[-7:]
    loads = load_pieces(refs[:n_pieces], pieces, piece_sems)
    q_loads = load_pieces(q_refs, queries, q_sems)
    acc[...] = in_ref[...] + other_ref[...]
    add_products(pieces, loads, kept, acc)
    docs = acc.shape[0]
    hi = acc[...].astype(BF16)
    pair[:docs, :] = hi
    pair[docs:, :] = (acc[...] - hi.astype(F32)).astype(BF16)
    height = queries.shape[1]
    for k in range(n_parts):
        q_loads[k].wait()
        place = lax.rem(lax.axis_index("corp") + n_parts - k, n_parts)
        both = dot_t(queries[k], pair[...])
        out_ref[pl.ds(pl.multiple_of(place * height, height), height), :] = both[:, :docs] + both[:, docs:]


VMEM = pl.BlockSpec(memory_space=pltpu.VMEM)
ANY = pl.BlockSpec(memory_space=pl.ANY)


def call(kernel, out_shape, operands, specs, scratch, flops, n_bytes, aliases):
    return pl.pallas_call(
        kernel,
        out_shape=out_shape,
        in_specs=specs,
        out_specs=jax.tree.map(lambda _: VMEM, out_shape),
        scratch_shapes=scratch,
        input_output_aliases=aliases,
        cost_estimate=pl.CostEstimate(flops=flops, bytes_accessed=n_bytes, transcendentals=0),
        compiler_params=pltpu.CompilerParams(vmem_limit_bytes=24 << 20),
    )(*operands)


def piece_scratch(pieces):
    return [pltpu.VMEM((len(pieces),) + pieces[0].shape, BF16), pltpu.SemaphoreType.DMA((len(pieces),))]


def apply(n, accs, kept, blocks, rows, m, keep):
    pieces = [p for b in blocks for p in b]
    sets = len(blocks[0])
    docs, span = pieces[0].shape
    depth = min(TILE_ROWS, span)
    shape = [jax.ShapeDtypeStruct((docs, m.shape[1]), F32)] * sets
    shape += [jax.ShapeDtypeStruct((span, m.shape[1]), BF16)] * (len(kept) + len(keep))
    carried = accs + kept
    scratch = piece_scratch(pieces) + [
        pltpu.VMEM((SLOTS, depth, m.shape[1]), BF16),
        pltpu.SemaphoreType.DMA((SLOTS,)),
        pltpu.SemaphoreType.DMA((max(1, len(keep)),)),
    ]
    outs = call(
        functools.partial(apply_kernel, n, rows, sets, bool(accs), len(kept), keep),
        shape,
        pieces + [m] + carried,
        [ANY] * (len(pieces) + 1) + [VMEM] * len(carried),
        scratch,
        2 * docs * len(pieces) * span * m.shape[1],
        2 * (len(rows) + len(keep)) * span * m.shape[1],
        {len(pieces) + 1 + k: k for k in range(len(carried))},
    )
    return list(outs[:sets]), list(outs[sets:])


def add(acc, kept, pieces):
    (acc,) = call(
        functools.partial(add_kernel, len(pieces)),
        [jax.ShapeDtypeStruct(acc.shape, F32)],
        pieces + kept + [acc],
        [ANY] * len(pieces) + [VMEM] * (len(kept) + 1),
        piece_scratch(pieces),
        2 * acc.shape[0] * len(kept) * kept[0].shape[0] * acc.shape[1],
        4 * acc.shape[0] * acc.shape[1],
        {len(pieces) + len(kept): 0},
    )
    return acc


def score(accs, kept, pieces, parts):
    queries = sum(p.shape[0] for p in parts)
    docs, width = accs[0].shape
    scratch = [
        pltpu.VMEM((docs, width), F32),
        pltpu.VMEM((2 * docs, width), BF16),
        *piece_scratch(parts),
        *piece_scratch(pieces),
    ]
    return call(
        functools.partial(score_kernel, len(pieces), len(parts)),
        jax.ShapeDtypeStruct((queries, docs), F32),
        pieces + accs + kept + parts,
        [ANY] * len(pieces) + [VMEM] * (2 + len(kept)) + [ANY] * len(parts),
        scratch,
        2 * docs * width * (2 * queries + len(pieces) * pieces[0].shape[1]),
        2 * queries * width,
        {},
    )


def scatter_sum(s, n, me):
    x, z, m = lax.rem(me, 2), lax.div(me, 2), n // 2
    s = s.reshape((m, 2) + s.shape[1:])
    mine = lax.dynamic_index_in_dim(s, x, 1, False)
    theirs = lax.dynamic_index_in_dim(s, 1 - x, 1, False)
    s = mine + lax.ppermute(theirs, "feat", [(i, i ^ 1) for i in range(n)])
    out = lax.dynamic_index_in_dim(s, z, 0, False)
    for k in range(1, m):
        y = lax.dynamic_index_in_dim(s, lax.rem(z + k, m), 0, False)
        out = out + lax.ppermute(y, "feat", [(i, (i + 2 * k) % n) for i in range(n)])
    return out


def ring_body(n, q, m, d):
    docs, width = d.shape
    half = width // 2
    far = n // 2
    order = ring_order(n)
    d, me, core = lax.optimization_barrier((d, lax.axis_index("feat"), lax.axis_index("corp")))

    def move(x, shift, cross):
        pairs = [
            (2 * order[p] + c, 2 * order[(p + shift(c)) % n] + (c ^ cross)) for p in range(n) for c in range(2)
        ]
        return lax.ppermute(x, ("feat", "corp"), pairs)

    def fore(c):
        return 1 - 2 * c

    def back(c):
        return 2 * c - 1

    p_fore = p_back = lax.dynamic_slice(d, (0, core * half), (docs, half))
    r_fore = r_back = lax.dynamic_slice(d, (0, (1 - core) * half), (docs, half))
    own_p = p_fore
    own_r = move(r_fore, lambda c: 0, 1)
    parts = [q, lax.ppermute(q, "corp", [(0, 1), (1, 0)])]
    accs, kept = [], []
    blocks, rows = [(own_p, own_r)], [(0, False)]
    keeps = {1: [(far, False), (far, True)], 2: [(n - far + 1, False), (far - 1, False)]}
    for s in range(1, far):
        r_ways = (back, fore) if s == 1 else (fore, back)
        r_fore = move(r_fore, r_ways[0], s == 1)
        r_back = move(r_back, r_ways[1], s == 1)
        p_fore, p_back = move(p_fore, fore, 0), move(p_back, back, 0)
        accs, kept = apply(n, accs, kept, blocks, rows, m, keeps.get(s, []))
        blocks, rows = [(p_fore, r_fore), (p_back, r_back)], [(n - s, False), (s, False)]

    mine, theirs = accs
    z_r, z_p = move(r_fore, fore, 1), move(p_fore, fore, 0)
    theirs = add(theirs, kept[2:], [r_fore, r_back])
    other = lax.ppermute(theirs, "corp", [(0, 1), (1, 0)])
    mine = add(mine, kept[2:], [p_fore, p_back])
    scores = score([mine, other], kept[:2], [z_p, z_r], parts)
    scores, me = lax.optimization_barrier((scores, me))
    return scatter_sum(scores.reshape(n, -1, docs), n, me)


def plain_body(q, m, d):
    applied = dot(lax.all_gather(d, "feat", axis=1, tiled=True), m)
    left = lax.all_gather(q, "corp", axis=0, tiled=True).astype(F32)
    scores = lax.dot_general(
        left, applied, (((1,), (1,)), ((), ())), precision=lax.Precision.HIGHEST, preferred_element_type=F32
    )
    return lax.psum_scatter(scores, "feat", scatter_dimension=0, tiled=True)


def solution(mesh):
    n, n_corp = mesh.shape["feat"], mesh.shape["corp"]
    ring = n % 4 == 0 and 8 <= n <= 16 and n_corp == 2

    def on_device(q, m, d):
        if not ring:
            return plain_body(q, m, d)
        return ring_body(n, q, m, d)

    placed = (P(("groups", "corp"), "feat"), P(None, "feat"), P(("groups", "corp"), "feat"))
    return jax.shard_map(
        on_device,
        mesh=mesh,
        in_specs=placed,
        out_specs=P(("groups", "feat"), "corp"),
        check_vma=False,
    )
```
